32 devices in a mesh: groups: 2 (over y), owners: 4 (over z), section: 2 (over x), rep: 2 (over core).
Axes of the slice: x: 2, y: 2, z: 4, core: 2. Of those that a mesh axis runs over, the one named last changes fastest.
Arguments:
- inputs: bfloat16 [2, 4096, 512], P('section', 'owners', ('groups', 'rep')), parts along dimension 2, may hold values from -6 to 6
- weight_first: bfloat16 [2, 32, 2048, 128], P('section', ('owners', 'rep')), may hold values from -0.1875 to 0.1875
- weight_second: bfloat16 [2, 32, 1024, 128], P('section', ('owners', 'rep')), may hold values from -0.25 to 0.25
- bias_first: float32 [2, 4096], P('section', 'owners'), may hold values from -1.5 to 1.5
- bias_second: float32 [2, 4096], P('section', 'owners'), may hold values from -1.5 to 1.5
- links_first: int32 [2, 32, 16], P('section', 'owners'), may hold values from 0 to 15, as said below
- links_second: int32 [2, 32, 8], P('section', 'owners'), may hold values from 0 to 7, as said below
Outputs:
- final_activity: bfloat16 [2, 4096, 512], P('section', 'owners', ('groups', 'rep')), parts along dimension 2
The draws below stay inside these ranges and needn't reach their ends.
There are 2 independent parts, one for each index of `groups`. The reference program is written for one: setup_inputs(seed, part) draws one part's arguments, and reference() takes and returns one part's arrays. A program takes and returns all parts, laid end to end along the dimension named above; an argument that names none is the same for every part. Nothing has to cross between parts.
Inputs may be any that keep to these rules, and one draw needn't show every extreme that they name: `links_first`: in every row of every section the 16 entries are distinct. `links_second`: in every row of every section the 8 entries are distinct.
All inputs are finite; a program needn't handle non-finite values.
Results may differ from the reference program's by a relative error of at most 0.014.
Values may be sent and summed in bfloat16 or wider, within the bound.
A program may use at most 64 MiB of HBM per device.

```python
import jax
import jax.numpy as jnp
from jax import lax

BLOCK = 128
RADIX_A = 16
RADIX_B = 8
NN = 4096
NB = 32
BATCH = 256
MICRO = 2
N_OWNERS = 4
N_SECTION = 2


def draw_links_first(key, part):
    key_list = jax.random.split(jax.random.fold_in(key, 11), N_SECTION * NB)
    shuffled = jax.vmap(lambda subkey: jax.random.permutation(subkey, RADIX_A))(key_list)
    return shuffled.reshape(N_SECTION, NB, RADIX_A).astype(jnp.int32)


def draw_links_second(key, part):
    key_list = jax.random.split(jax.random.fold_in(key, 23), N_SECTION * NB)
    shuffled = jax.vmap(lambda subkey: jax.random.permutation(subkey, RADIX_B))(key_list)
    return shuffled.reshape(N_SECTION, NB, RADIX_B).astype(jnp.int32)


def level_of(own_key, dims, cuts, smallest, high):
    loudness = 1.0
    for dim, parts in cuts:
        draws = jax.random.uniform(jax.random.fold_in(jax.random.fold_in(own_key, 6), dim), (parts,), jnp.float32, smallest / len(cuts), high / len(cuts))
        loudness = loudness * jnp.repeat(jnp.exp(draws), dims[dim] // parts).reshape((-1,) + (1,) * (len(dims) - 1 - dim))
    return loudness


def scatter_about(stream_key, extent, width, limit, cuts=(), kind=jnp.bfloat16):
    array = width * jax.random.normal(stream_key, extent, jnp.float32)
    if cuts:
        array = array * level_of(stream_key, extent, cuts, -0.22, 0.18)
    return jnp.clip(array, -limit, limit).astype(kind)


def setup_inputs(seed: int = 0, part: int = 0) -> dict:
    key_of = jax.random.split(jax.random.key(seed), 8)
    part_splits = jax.random.split(jax.random.fold_in(key_of[7], part), 8)
    inputs = scatter_about(part_splits[0], (MICRO, NN, BATCH), 1.0, 6.0, ((0, 2), (1, 4), (2, 2)))
    weight_first = scatter_about(key_of[1], (N_SECTION, NB, RADIX_A * BLOCK, BLOCK), (RADIX_A * BLOCK // 2) ** -0.5, 0.1875, ((0, 2), (1, 8)))
    weight_second = scatter_about(key_of[2], (N_SECTION, NB, RADIX_B * BLOCK, BLOCK), (RADIX_B * BLOCK // 2) ** -0.5, 0.25, ((0, 2), (1, 8)))
    bias_first = scatter_about(key_of[3], (N_SECTION, NN), 0.3, 1.5, ((0, 2), (1, 4)), jnp.float32)
    bias_second = scatter_about(key_of[4], (N_SECTION, NN), 0.3, 1.5, ((0, 2), (1, 4)), jnp.float32)
    links_first = draw_links_first(jax.random.fold_in(key_of[7], 71), part)
    links_second = draw_links_second(jax.random.fold_in(key_of[7], 71), part)
    return {"inputs": inputs, "weight_first": weight_first, "weight_second": weight_second, "bias_first": bias_first, "bias_second": bias_second, "links_first": links_first, "links_second": links_second}


CEILING = 4.0


def regroup(activity):
    owner_width = activity.shape[0] // N_OWNERS
    piece_len = owner_width // N_OWNERS
    batch_len = activity.shape[1]
    shaped = activity.reshape(N_OWNERS, N_OWNERS, piece_len, batch_len)
    return jnp.transpose(shaped, (1, 0, 2, 3)).reshape(activity.shape)


def radix_layer(activity, tiles, link_table, bias_row):
    radix_len = link_table.shape[1]
    groups_total = link_table.shape[0] // radix_len
    tile_size = tiles.shape[2]
    batch_len = activity.shape[1]
    grouped_act = activity.reshape(groups_total, radix_len, tile_size, batch_len)
    grouped_tiles = tiles.reshape(groups_total, radix_len, radix_len * tile_size, tile_size)
    grouped_links = link_table.reshape(groups_total, radix_len, radix_len)
    grouped_bias = bias_row.reshape(groups_total, radix_len, tile_size)

    def one_group(packed):
        blocks, tile_group, link_group, bias_group = packed
        picked = jnp.take(blocks, link_group, axis=0)
        picked = picked.reshape(radix_len, radix_len * tile_size, batch_len).astype(jnp.float32)
        summed = jnp.einsum("bkc,bkr->bcr", tile_group.astype(jnp.float32), picked,
                            precision=lax.Precision.HIGHEST)
        summed = summed + bias_group[:, :, None]
        return jnp.clip(summed, 0.0, CEILING).astype(jnp.bfloat16)

    mapped = lax.map(one_group, (grouped_act, grouped_tiles, grouped_links, grouped_bias))
    return mapped.reshape(link_table.shape[0] * tile_size, batch_len)


def reference(inputs, weight_first, weight_second, bias_first, bias_second, links_first, links_second):
    results = []
    for micro_idx in range(MICRO):
        activity = inputs[micro_idx]
        for section_pos in range(N_SECTION):
            activity = radix_layer(regroup(activity), weight_first[section_pos], links_first[section_pos], bias_first[section_pos])
            activity = radix_layer(regroup(activity), weight_second[section_pos], links_second[section_pos], bias_second[section_pos])
        results.append(activity)
    return jnp.stack(results)
```

```python
import functools

import jax
import jax.numpy as jnp
from jax import lax
from jax.experimental import pallas as pl
from jax.experimental.pallas import tpu as pltpu
from jax.sharding import PartitionSpec as P

CEILING = 4.0
MESH = pl.DeviceIdType.MESH


def relay(dims, x, w1, w2, b1_in, b2_in, l1_in, l2_in, o, b1, b2, l1, l2, raw1, far1, raw2, far2, til1, til2, col1, col2,
          in_a, in_b, mid, res, via, s_w, r_w, l_w, s_in, s_a, r_a, s_f, s_b, r_b, s_o, r_o, s_v, r_v, ready):
    n, sections, span, tile = dims
    me = lax.axis_index("owners")
    sec = lax.axis_index("section")
    rep = lax.axis_index("rep")
    piece = x.shape[1]
    width = n * piece
    rows = x.shape[2]
    blocks = width // tile
    half = w1.shape[0]
    last = sections - 1

    barrier = pltpu.get_barrier_semaphore()
    par = lax.rem(me, span)
    base = me - par
    classes = n // span

    def fellow(k):
        return lax.rem(me + span * k, n)

    def mate(j):
        return base + lax.rem(par + j, span)

    def greet(sem, w, t):
        pl.semaphore_signal(sem, inc=1, device_id={"owners": w, "section": t}, device_id_type=MESH)

    near = [fellow(k) for k in range(1, classes)] + [mate(j) for j in range(1, span)]

    @pl.when(sec == 0)
    def _():
        for w in near:
            greet(barrier, w, 0)
    for t in range(1, sections):
        for w in range(n):
            @pl.when(jnp.logical_or(me != w, sec != t))
            def _():
                greet(barrier, w, t)
    pl.semaphore_signal(barrier, inc=1, device_id={"rep": 1 - rep}, device_id_type=MESH)

    local = [
        pltpu.make_async_copy(w1, raw1, l_w.at[0]),
        pltpu.make_async_copy(w2, raw2, l_w.at[1]),
        pltpu.make_async_copy(l1_in, l1, l_w.at[2]),
        pltpu.make_async_copy(l2_in, l2, l_w.at[3]),
        pltpu.make_async_copy(b1_in, b1, l_w.at[4]),
        pltpu.make_async_copy(b2_in, b2, l_w.at[5]),
    ]
    for copy in local:
        copy.start()
    @pl.when(sec == 0)
    def _():
        pl.semaphore_wait(barrier, len(near) + 1)

    @pl.when(sec != 0)
    def _():
        pl.semaphore_wait(barrier, n * sections)

    @pl.when(sec == 1)
    def _():
        for k in range(classes):
            greet(ready, fellow(k), 0)

    bytes_of = in_a.at[0, 0, 0]

    def send_a(src, slot, h, w, target, sem):
        pltpu.make_async_remote_copy(
            src_ref=src.at[(w // span) * span + h], dst_ref=in_a.at[slot, h, me],
            send_sem=sem.at[h, w], recv_sem=r_a.at[slot, h, me],
            device_id={"owners": w, "section": target}, device_id_type=MESH).start()

    def done(sem):
        pltpu.make_async_copy(bytes_of, bytes_of, sem).wait()

    def done_piece(sem):
        pltpu.make_async_copy(via.at[0], via.at[0], sem).wait()

    @pl.when(sec == 0)
    def _():
        for w in near:
            for h in range(span):
                send_a(x, 0, h, w, 0, s_in)
        for h in range(span):
            pltpu.make_async_copy(x.at[base + h], in_a.at[0, h, me], r_a.at[0, h, me]).start()

    @pl.when(sec != 0)
    def _():
        for d in range(n - 1, -1, -1):
            for h in range(span):
                send_a(x, sec + 1, h, lax.rem(me + d, n), 0, s_in)

    def weight_copy(src, dst, k):
        return pltpu.make_async_remote_copy(
            src_ref=src, dst_ref=dst,
            send_sem=s_w.at[k], recv_sem=r_w.at[k],
            device_id={"rep": 1 - rep}, device_id_type=MESH)

    weight_copy(w1, far1, 0).start()
    weight_copy(w2, far2, 1).start()

    def arrange(raw, til, links, begin, spans):
        radix = spans * blocks

        def one(b, carry):
            i = b + begin
            taken = [links[i, k] for k in range(radix)]
            for p in range(radix):
                slot = jnp.int32(0)
                for k in range(1, radix):
                    slot = jnp.where(taken[k] == p, k, slot)
                til[pl.ds(pl.multiple_of(i * tile, tile), tile), p * tile:(p + 1) * tile] = raw[b, slot].T
            return carry

        lax.fori_loop(0, half, one, 0)

    def bias_columns(b, col):
        for i in range(blocks):
            row = b[0:1, i * tile:(i + 1) * tile]
            col[i * tile:(i + 1) * tile, :] = jnp.broadcast_to(row, (rows, tile)).T

    for copy in local[2:]:
        copy.wait()
    bias_columns(b1, col1)
    bias_columns(b2, col2)
    local[0].wait()
    arrange(raw1, til1, l1, rep * half, span)
    weight_copy(w1, far1, 0).wait_recv()
    arrange(far1, til1, l1, (1 - rep) * half, span)

    def slab(ref, w):
        return ref[pl.ds(pl.multiple_of(w * piece, piece), piece), :]

    def product(til, v, col, w):
        part = jnp.dot(slab(til, w), v, preferred_element_type=jnp.float32)
        return jnp.clip(part + slab(col, w), 0.0, CEILING).astype(jnp.bfloat16)

    def far(d):
        low, high = me, n - 1 - me
        short = jnp.minimum(low, high)
        k = n - 1 - d
        both = (k + 1) // 2
        away = jnp.where(k <= 2 * short, both, k - short)
        up = jnp.where(k <= 2 * short, (k % 2) == 0, high > low)
        return jnp.where(up, me + away, me - away)

    def slot_of(m):
        return jnp.where(sec == 0, 0, 1) if m == 0 else m + 1

    def forward(m, h, u, j):
        slot = slot_of(m)
        return pltpu.make_async_remote_copy(
            src_ref=in_a.at[slot, h, u], dst_ref=in_a.at[slot, h, u],
            send_sem=s_f.at[m, h, u, j - 1], recv_sem=r_a.at[slot, h, u],
            device_id={"owners": mate(j)}, device_id_type=MESH)

    def relayed(m, k, act):
        if m == last:
            if m == 0 and k > 0:
                pl.when(sec == 0)(act)
        elif m == 0 and k > 0:
            act()
        else:
            pl.when(sec > 0)(act)

    def forwards(m, act):
        for k in range(classes):
            def go():
                for h in range(span):
                    for j in range(1, span):
                        act(forward(m, h, fellow(k), j))
            relayed(m, k, go)

    def first_layer(m):
        slot = slot_of(m)
        for k in range(classes):
            u = fellow(k)
            for h in range(span):
                done(r_a.at[slot, h, u])

                def go():
                    for j in range(1, span):
                        forward(m, h, u, j).start()
                relayed(m, k, go)
        for j in range(1, span):
            for k in range(classes):
                for h in range(span):
                    done(r_a.at[slot, h, lax.rem(mate(j) + span * k, n)])
        v = in_a[slot].reshape(span * width, rows)
        for d in range(n):
            w = far(d)
            mid[m, w] = product(til1, v, col1, w)
            if d < n - 1:
                def straight():
                    pltpu.make_async_remote_copy(
                        src_ref=mid.at[m, w], dst_ref=in_b.at[m, me],
                        send_sem=s_b.at[m, d + 1], recv_sem=r_b.at[m, me],
                        device_id={"owners": w}, device_id_type=MESH).start()

                def detour():
                    pltpu.make_async_remote_copy(
                        src_ref=mid.at[m, w], dst_ref=via.at[w],
                        send_sem=s_b.at[m, d + 1], recv_sem=r_v.at[w],
                        device_id={"section": 1}, device_id_type=MESH).start()

                if m == 1:
                    pl.when(sec == 0)(detour)
                    pl.when(sec > 0)(straight)
                else:
                    straight()
            else:
                in_b[m, me] = mid[m, me]

    def second_layer(m):
        for d in range(1, n):
            done(r_b.at[m, lax.rem(me + d, n)])
        v = in_b[m].reshape(width, rows)
        for w in range(n):
            res[m, w] = product(til2, v, col2, w)

        if last > 0:
            @pl.when(sec < last)
            def _():
                for d in (range(n - 1, -1, -1) if m == last else range(n - span, -1, -span)):
                    for h in range(span):
                        send_a(res.at[m], m + 1, h, lax.rem(me + d, n), sec + 1, s_a.at[m])

        @pl.when(sec == last)
        def _():
            if m == last:
                o[...] = res[m]
            else:
                pltpu.make_async_remote_copy(
                    src_ref=res.at[m], dst_ref=o, send_sem=s_o.at[m], recv_sem=r_o.at[0],
                    device_id={"section": m}, device_id_type=MESH).start()

    def arrange_second():
        local[1].wait()
        arrange(raw2, til2, l2, rep * half, 1)
        weight_copy(w2, far2, 1).wait_recv()
        arrange(far2, til2, l2, (1 - rep) * half, 1)

    def onward(w):
        return pltpu.make_async_remote_copy(
            src_ref=via.at[w], dst_ref=in_b.at[1, me], send_sem=s_v.at[w], recv_sem=r_b.at[1, me],
            device_id={"owners": w, "section": 0}, device_id_type=MESH)

    @pl.when(sec > 0)
    def _():
        arrange_second()

    if last > 0:
        @pl.when(sec == 1)
        def _():
            for d in range(n - 1):
                w = far(d)
                done_piece(r_v.at[w])
                onward(w).start()

    first_layer(0)

    @pl.when(sec == 0)
    def _():
        arrange_second()

    if last > 0:
        @pl.when(sec == 0)
        def _():
            pl.semaphore_wait(ready, classes)

    for m in range(sections):
        if m < last:
            @pl.when(sec == 0)
            def _():
                first_layer(m + 1)
        second_layer(m)
        if m < last:
            @pl.when(sec > 0)
            def _():
                first_layer(m + 1)

    def sent(ref, sem):
        pltpu.make_async_copy(ref, ref, sem).wait()

    @pl.when(sec == 0)
    def _():
        for w in near:
            for h in range(span):
                done(s_in.at[h, w])

    @pl.when(sec != 0)
    def _():
        for w in range(n):
            for h in range(span):
                done(s_in.at[h, w])
    for m in range(sections):
        forwards(m, lambda copy: copy.wait_send())
        for d in range(1, n):
            sent(mid.at[m, 0], s_b.at[m, d])
    weight_copy(w1, far1, 0).wait_send()
    weight_copy(w2, far2, 1).wait_send()
    if last > 0:
        @pl.when(sec == 1)
        def _():
            for d in range(n - 1):
                onward(far(d)).wait_send()

        @pl.when(sec < last)
        def _():
            for m in range(sections):
                for d in range(0, n, 1 if m == last else span):
                    for h in range(span):
                        done(s_a.at[m, h, lax.rem(me + d, n)])
            sent(o, r_o.at[0])

        @pl.when(sec == last)
        def _():
            for m in range(last):
                sent(res.at[m], s_o.at[m])


def body(inputs, weight_first, weight_second, bias_first, bias_second, links_first, links_second):
    n = lax.axis_size("owners")
    sections = lax.axis_size("section")
    width, rows = inputs.shape[1:]
    half, deep, tile = weight_first.shape[1:]
    radix_a = links_first.shape[2]
    radix_b = links_second.shape[2]
    blocks = width // tile
    span = radix_a // blocks
    piece = width // n
    dims = (n, sections, span, tile)
    bf = jnp.bfloat16
    anyspace = pl.BlockSpec(memory_space=pltpu.HBM)
    vmem = pl.BlockSpec(memory_space=pltpu.VMEM)
    dma = pltpu.SemaphoreType.DMA
    out = pl.pallas_call(
        functools.partial(relay, dims),
        name="relay",
        out_shape=jax.ShapeDtypeStruct((n, piece, rows), bf),
        in_specs=[anyspace] * 7,
        out_specs=vmem,
        scratch_shapes=[
            pltpu.VMEM(bias_first.shape, jnp.float32),
            pltpu.VMEM(bias_second.shape, jnp.float32),
            pltpu.SMEM(links_first.shape[1:], jnp.int32),
            pltpu.SMEM(links_second.shape[1:], jnp.int32),
            pltpu.VMEM((half, radix_a, tile, tile), bf),
            pltpu.VMEM((half, radix_a, tile, tile), bf),
            pltpu.VMEM((half, radix_b, tile, tile), bf),
            pltpu.VMEM((half, radix_b, tile, tile), bf),
            pltpu.VMEM((width, radix_a * tile), bf),
            pltpu.VMEM((width, radix_b * tile), bf),
            pltpu.VMEM((width, rows), jnp.float32),
            pltpu.VMEM((width, rows), jnp.float32),
            pltpu.VMEM((sections + 1, span, n, piece, rows), bf),
            pltpu.VMEM((sections, n, piece, rows), bf),
            pltpu.VMEM((sections, n, piece, rows), bf),
            pltpu.VMEM((sections, n, piece, rows), bf),
            pltpu.VMEM((n, piece, rows), bf),
            dma((2,)), dma((2,)), dma((6,)),
            dma((span, n)), dma((sections, span, n)), dma((sections + 1, span, n)),
            dma((sections, span, n, max(span - 1, 1))),
            dma((sections, n)), dma((sections, n)),
            dma((sections,)), dma((1,)), dma((n,)), dma((n,)), pltpu.SemaphoreType.REGULAR,
        ],
        compiler_params=pltpu.CompilerParams(
            collective_id=0, has_side_effects=True, vmem_limit_bytes=67043328),
    )(
        inputs.reshape(n, piece, rows),
        weight_first.reshape(half, radix_a, tile, tile),
        weight_second.reshape(half, radix_b, tile, tile),
        bias_first, bias_second, links_first[0], links_second[0],
    )
    return out.reshape(1, width, rows)


def solution(mesh):
    placed = (
        P("section", "owners", ("groups", "rep")),
        P("section", ("owners", "rep"), None, None),
        P("section", ("owners", "rep"), None, None),
        P("section", "owners"),
        P("section", "owners"),
        P("section", "owners", None),
        P("section", "owners", None),
    )
    return jax.shard_map(
        body,
        mesh=mesh,
        in_specs=placed,
        out_specs=P("section", "owners", ("groups", "rep")),
        check_vma=False,
    )
```

```python
import functools

import jax
import jax.numpy as jnp
from jax import lax
from jax.experimental import pallas as pl
from jax.experimental.pallas import tpu as pltpu
from jax.sharding import PartitionSpec as P

CEILING = 4.0
MESH = pl.DeviceIdType.MESH


def relay(dims, x, w1, w2, b1_in, b2_in, l1_in, l2_in, o, b1, b2, l1, l2, raw1, far1, raw2, far2, til1, til2, col1, col2,
          in_a, in_b, mid, res, via, s_w, r_w, l_w, s_in, s_a, r_a, s_f, s_b, r_b, s_o, r_o, s_v, r_v, ready):
    n, sections, span, tile = dims
    me = lax.axis_index("owners")
    sec = lax.axis_index("section")
    rep = lax.axis_index("rep")
    piece = x.shape[1]
    width = n * piece
    rows = x.shape[2]
    blocks = width // tile
    half = w1.shape[0]
    last = sections - 1

    barrier = pltpu.get_barrier_semaphore()
    par = lax.rem(me, span)
    base = me - par
    classes = n // span

    def fellow(k):
        return lax.rem(me + span * k, n)

    def mate(j):
        return base + lax.rem(par + j, span)

    def greet(sem, w, t):
        pl.semaphore_signal(sem, inc=1, device_id={"owners": w, "section": t}, device_id_type=MESH)

    near = [fellow(k) for k in range(1, classes)] + [mate(j) for j in range(1, span)]

    @pl.when(sec == 0)
    def _():
        for w in near:
            greet(barrier, w, 0)
    for t in range(1, sections):
        for w in range(n):
            @pl.when(jnp.logical_or(me != w, sec != t))
            def _():
                greet(barrier, w, t)
    pl.semaphore_signal(barrier, inc=1, device_id={"rep": 1 - rep}, device_id_type=MESH)

    local = [
        pltpu.make_async_copy(w1, raw1, l_w.at[0]),
        pltpu.make_async_copy(w2, raw2, l_w.at[1]),
        pltpu.make_async_copy(l1_in, l1, l_w.at[2]),
        pltpu.make_async_copy(l2_in, l2, l_w.at[3]),
        pltpu.make_async_copy(b1_in, b1, l_w.at[4]),
        pltpu.make_async_copy(b2_in, b2, l_w.at[5]),
    ]
    for copy in local:
        copy.start()
    @pl.when(sec == 0)
    def _():
        pl.semaphore_wait(barrier, len(near) + 1)

    @pl.when(sec != 0)
    def _():
        pl.semaphore_wait(barrier, n * sections)

    @pl.when(sec == 1)
    def _():
        for k in range(classes):
            greet(ready, fellow(k), 0)

    bytes_of = in_a.at[0, 0, 0]

    def send_a(src, slot, h, w, target, sem):
        pltpu.make_async_remote_copy(
            src_ref=src.at[(w // span) * span + h], dst_ref=in_a.at[slot, h, me],
            send_sem=sem.at[h, w], recv_sem=r_a.at[slot, h, me],
            device_id={"owners": w, "section": target}, device_id_type=MESH).start()

    def done(sem):
        pltpu.make_async_copy(bytes_of, bytes_of, sem).wait()

    def done_piece(sem):
        pltpu.make_async_copy(via.at[0], via.at[0], sem).wait()

    @pl.when(sec == 0)
    def _():
        for w in near:
            for h in range(span):
                send_a(x, 0, h, w, 0, s_in)
        for h in range(span):
            pltpu.make_async_copy(x.at[base + h], in_a.at[0, h, me], r_a.at[0, h, me]).start()

    @pl.when(sec != 0)
    def _():
        for d in range(n - 1, -1, -1):
            for h in range(span):
                send_a(x, sec + 1, h, lax.rem(me + d, n), 0, s_in)

    def weight_copy(src, dst, k):
        return pltpu.make_async_remote_copy(
            src_ref=src, dst_ref=dst,
            send_sem=s_w.at[k], recv_sem=r_w.at[k],
            device_id={"rep": 1 - rep}, device_id_type=MESH)

    weight_copy(w1, far1, 0).start()
    weight_copy(w2, far2, 1).start()

    def arrange(raw, til, links, begin, spans):
        radix = spans * blocks

        def one(b, carry):
            i = b + begin
            taken = [links[i, k] for k in range(radix)]
            for p in range(radix):
                slot = jnp.int32(0)
                for k in range(1, radix):
                    slot = jnp.where(taken[k] == p, k, slot)
                til[pl.ds(pl.multiple_of(i * tile, tile), tile), p * tile:(p + 1) * tile] = raw[b, slot].T
            return carry

        lax.fori_loop(0, half, one, 0)

    def bias_columns(b, col):
        for i in range(blocks):
            row = b[0:1, i * tile:(i + 1) * tile]
            col[i * tile:(i + 1) * tile, :] = jnp.broadcast_to(row, (rows, tile)).T

    for copy in local[2:]:
        copy.wait()
    bias_columns(b1, col1)
    bias_columns(b2, col2)
    local[0].wait()
    arrange(raw1, til1, l1, rep * half, span)
    weight_copy(w1, far1, 0).wait_recv()
    arrange(far1, til1, l1, (1 - rep) * half, span)

    def slab(ref, w):
        return ref[pl.ds(pl.multiple_of(w * piece, piece), piece), :]

    def product(til, v, col, w):
        part = jnp.dot(slab(til, w), v, preferred_element_type=jnp.float32)
        return jnp.clip(part + slab(col, w), 0.0, CEILING).astype(jnp.bfloat16)

    def far(d):
        low, high = me, n - 1 - me
        short = jnp.minimum(low, high)
        k = n - 1 - d
        both = (k + 1) // 2
        away = jnp.where(k <= 2 * short, both, k - short)
        up = jnp.where(k <= 2 * short, (k % 2) == 0, high > low)
        return jnp.where(up, me + away, me - away)

    def slot_of(m):
        return jnp.where(sec == 0, 0, 1) if m == 0 else m + 1

    def forward(m, h, u, j):
        slot = slot_of(m)
        return pltpu.make_async_remote_copy(
            src_ref=in_a.at[slot, h, u], dst_ref=in_a.at[slot, h, u],
            send_sem=s_f.at[m, h, u, j - 1], recv_sem=r_a.at[slot, h, u],
            device_id={"owners": mate(j)}, device_id_type=MESH)

    def relayed(m, k, act):
        if m == last:
            if m == 0 and k > 0:
                pl.when(sec == 0)(act)
        elif m == 0 and k > 0:
            act()
        else:
            pl.when(sec > 0)(act)

    def forwards(m, act):
        for k in range(classes):
            def go():
                for h in range(span):
                    for j in range(1, span):
                        act(forward(m, h, fellow(k), j))
            relayed(m, k, go)

    def first_layer(m):
        slot = slot_of(m)
        def pull(u, passing):
            for h in range(span):
                done(r_a.at[slot, h, u])
                if passing:
                    for j in range(1, span):
                        forward(m, h, u, j).start()

        @pl.when(sec == 0)
        def _():
            for k in range(classes):
                pull(fellow(k), m == 0 and k > 0)

        @pl.when(sec > 0)
        def _():
            edge = jnp.logical_or(me == 0, me == n - 1)
            for k in range(classes):
                pull(fellow(jnp.where(edge, k, classes - 1 - k)), m < last)

        for j in range(1, span):
            for k in range(classes):
                for h in range(span):
                    done(r_a.at[slot, h, lax.rem(mate(j) + span * k, n)])
        v = in_a[slot].reshape(span * width, rows)
        for d in range(n):
            w = far(d)
            mid[m, w] = product(til1, v, col1, w)
            if d < n - 1:
                def straight():
                    pltpu.make_async_remote_copy(
                        src_ref=mid.at[m, w], dst_ref=in_b.at[m, me],
                        send_sem=s_b.at[m, d + 1], recv_sem=r_b.at[m, me],
                        device_id={"owners": w}, device_id_type=MESH).start()

                def detour():
                    pltpu.make_async_remote_copy(
                        src_ref=mid.at[m, w], dst_ref=via.at[w],
                        send_sem=s_b.at[m, d + 1], recv_sem=r_v.at[w],
                        device_id={"section": 1}, device_id_type=MESH).start()

                if m == 1:
                    pl.when(sec == 0)(detour)
                    pl.when(sec > 0)(straight)
                else:
                    straight()
            else:
                in_b[m, me] = mid[m, me]

    def home(m, first):
        part = pl.ds(first, span)
        return pltpu.make_async_remote_copy(
            src_ref=res.at[m, part], dst_ref=o.at[part], send_sem=s_o.at[m, first // span], recv_sem=r_o.at[first // span],
            device_id={"section": m}, device_id_type=MESH)

    def second_layer(m):
        for d in range(1, n):
            done(r_b.at[m, lax.rem(me + d, n)])
        v = in_b[m].reshape(width, rows)
        for d in range(n - span, -1, -span):
            w = lax.rem(me + d, n)
            first = w - lax.rem(w, span)
            for h in range(span):
                value = product(til2, v, col2, first + h)
                res[m, first + h] = value
                if m == last:
                    @pl.when(sec == last)
                    def _():
                        o[first + h] = value

            if last > 0:
                @pl.when(sec < last)
                def _():
                    for j in range(span if m == last else 1):
                        for h in range(span):
                            send_a(res.at[m], m + 1, h, first + lax.rem(w - first + j, span), sec + 1, s_a.at[m])

            if m < last:
                @pl.when(sec == last)
                def _():
                    home(m, first).start()

    def arrange_second():
        local[1].wait()
        arrange(raw2, til2, l2, rep * half, 1)
        weight_copy(w2, far2, 1).wait_recv()
        arrange(far2, til2, l2, (1 - rep) * half, 1)

    def onward(w):
        return pltpu.make_async_remote_copy(
            src_ref=via.at[w], dst_ref=in_b.at[1, me], send_sem=s_v.at[w], recv_sem=r_b.at[1, me],
            device_id={"owners": w, "section": 0}, device_id_type=MESH)

    @pl.when(sec > 0)
    def _():
        arrange_second()

    if last > 0:
        @pl.when(sec == 1)
        def _():
            for d in range(n - 1):
                w = far(d)
                done_piece(r_v.at[w])
                onward(w).start()

    first_layer(0)

    if last > 0:
        @pl.when(sec == 0)
        def _():
            pl.semaphore_wait(ready, classes)

    for m in range(sections):
        if m < last:
            @pl.when(sec == 0)
            def _():
                first_layer(m + 1)
        if m == 0:
            @pl.when(sec == 0)
            def _():
                arrange_second()
        second_layer(m)
        if m < last:
            @pl.when(sec > 0)
            def _():
                first_layer(m + 1)

    def sent(ref, sem):
        pltpu.make_async_copy(ref, ref, sem).wait()

    @pl.when(sec == 0)
    def _():
        for w in near:
            for h in range(span):
                done(s_in.at[h, w])

    @pl.when(sec != 0)
    def _():
        for w in range(n):
            for h in range(span):
                done(s_in.at[h, w])
    for m in range(sections):
        forwards(m, lambda copy: copy.wait_send())
        for d in range(1, n):
            sent(mid.at[m, 0], s_b.at[m, d])
    weight_copy(w1, far1, 0).wait_send()
    weight_copy(w2, far2, 1).wait_send()
    if last > 0:
        @pl.when(sec == 1)
        def _():
            for d in range(n - 1):
                onward(far(d)).wait_send()

        @pl.when(sec < last)
        def _():
            for m in range(sections):
                for d in range(0, n, 1 if m == last else span):
                    for h in range(span):
                        done(s_a.at[m, h, lax.rem(me + d, n)])
            for k in range(classes):
                sent(o.at[pl.ds(0, span)], r_o.at[k])

        @pl.when(sec == last)
        def _():
            for m in range(last):
                for k in range(classes):
                    home(m, k * span).wait_send()


def body(inputs, weight_first, weight_second, bias_first, bias_second, links_first, links_second):
    n = lax.axis_size("owners")
    sections = lax.axis_size("section")
    width, rows = inputs.shape[1:]
    half, deep, tile = weight_first.shape[1:]
    radix_a = links_first.shape[2]
    radix_b = links_second.shape[2]
    blocks = width // tile
    span = radix_a // blocks
    piece = width // n
    dims = (n, sections, span, tile)
    bf = jnp.bfloat16
    anyspace = pl.BlockSpec(memory_space=pltpu.HBM)
    vmem = pl.BlockSpec(memory_space=pltpu.VMEM)
    dma = pltpu.SemaphoreType.DMA
    out = pl.pallas_call(
        functools.partial(relay, dims),
        name="relay",
        out_shape=pltpu.VMEM((n, piece, rows), bf),
        in_specs=[anyspace] * 7,
        out_specs=vmem,
        scratch_shapes=[
            pltpu.VMEM(bias_first.shape, jnp.float32),
            pltpu.VMEM(bias_second.shape, jnp.float32),
            pltpu.SMEM(links_first.shape[1:], jnp.int32),
            pltpu.SMEM(links_second.shape[1:], jnp.int32),
            pltpu.VMEM((half, radix_a, tile, tile), bf),
            pltpu.VMEM((half, radix_a, tile, tile), bf),
            pltpu.VMEM((half, radix_b, tile, tile), bf),
            pltpu.VMEM((half, radix_b, tile, tile), bf),
            pltpu.VMEM((width, radix_a * tile), bf),
            pltpu.VMEM((width, radix_b * tile), bf),
            pltpu.VMEM((width, rows), jnp.float32),
            pltpu.VMEM((width, rows), jnp.float32),
            pltpu.VMEM((sections + 1, span, n, piece, rows), bf),
            pltpu.VMEM((sections, n, piece, rows), bf),
            pltpu.VMEM((sections, n, piece, rows), bf),
            pltpu.VMEM((sections, n, piece, rows), bf),
            pltpu.VMEM((n, piece, rows), bf),
            dma((2,)), dma((2,)), dma((6,)),
            dma((span, n)), dma((sections, span, n)), dma((sections + 1, span, n)),
            dma((sections, span, n, max(span - 1, 1))),
            dma((sections, n)), dma((sections, n)),
            dma((sections, n // span)), dma((n // span,)), dma((n,)), dma((n,)), pltpu.SemaphoreType.REGULAR,
        ],
        compiler_params=pltpu.CompilerParams(
            collective_id=0, has_side_effects=True, vmem_limit_bytes=63 * 2 ** 20 + 2 ** 19),
    )(
        inputs.reshape(n, piece, rows),
        weight_first.reshape(half, radix_a, tile, tile),
        weight_second.reshape(half, radix_b, tile, tile),
        bias_first, bias_second, links_first[0], links_second[0],
    )
    return out.reshape(1, width, rows)


def solution(mesh):
    placed = (
        P("section", "owners", ("groups", "rep")),
        P("section", ("owners", "rep"), None, None),
        P("section", ("owners", "rep"), None, None),
        P("section", "owners"),
        P("section", "owners"),
        P("section", "owners", None),
        P("section", "owners", None),
    )
    return jax.shard_map(
        body,
        mesh=mesh,
        in_specs=placed,
        out_specs=P("section", "owners", ("groups", "rep")),
        check_vma=False,
    )
```

```python
import functools

import jax
import jax.numpy as jnp
from jax import lax
from jax.experimental import pallas as pl
from jax.experimental.pallas import tpu as pltpu
from jax.sharding import PartitionSpec as P

CEILING = 4.0
MESH = pl.DeviceIdType.MESH


def relay(dims, x, w1, w2, b1_in, b2_in, l1_in, l2_in, o, b1, b2, l1, l2, raw1, far1, raw2, far2, til1, til2, col1, col2,
          in_a, in_b, mid, res, via, s_w, r_w, l_w, s_in, s_a, r_a, s_f, s_b, r_b, s_o, r_o, s_v, r_v, ready):
    n, sections, span, tile = dims
    me = lax.axis_index("owners")
    sec = lax.axis_index("section")
    rep = lax.axis_index("rep")
    piece = x.shape[1]
    width = n * piece
    rows = x.shape[2]
    blocks = width // tile
    half = w1.shape[0]
    last = sections - 1

    barrier = pltpu.get_barrier_semaphore()
    par = lax.rem(me, span)
    base = me - par
    classes = n // span

    def fellow(k):
        return lax.rem(me + span * k, n)

    def mate(j):
        return base + lax.rem(par + j, span)

    def greet(sem, w, t):
        pl.semaphore_signal(sem, inc=1, device_id={"owners": w, "section": t}, device_id_type=MESH)

    near = [fellow(k) for k in range(1, classes)] + [mate(j) for j in range(1, span)]

    @pl.when(sec == 0)
    def _():
        for w in near:
            greet(barrier, w, 0)
    for t in range(1, sections):
        for w in range(n):
            @pl.when(jnp.logical_or(me != w, sec != t))
            def _():
                greet(barrier, w, t)
    pl.semaphore_signal(barrier, inc=1, device_id={"rep": 1 - rep}, device_id_type=MESH)

    local = [
        pltpu.make_async_copy(w1, raw1, l_w.at[0]),
        pltpu.make_async_copy(w2, raw2, l_w.at[1]),
        pltpu.make_async_copy(l1_in, l1, l_w.at[2]),
        pltpu.make_async_copy(l2_in, l2, l_w.at[3]),
        pltpu.make_async_copy(b1_in, b1, l_w.at[4]),
        pltpu.make_async_copy(b2_in, b2, l_w.at[5]),
    ]
    for copy in local:
        copy.start()
    @pl.when(sec == 0)
    def _():
        pl.semaphore_wait(barrier, len(near) + 1)

    @pl.when(sec != 0)
    def _():
        pl.semaphore_wait(barrier, n * sections)

    @pl.when(sec == 1)
    def _():
        for k in range(classes):
            greet(ready, fellow(k), 0)

    bytes_of = in_a.at[0, 0, 0]

    def send_a(src, slot, h, w, target, sem):
        pltpu.make_async_remote_copy(
            src_ref=src.at[(w // span) * span + h], dst_ref=in_a.at[slot, h, me],
            send_sem=sem.at[h, w], recv_sem=r_a.at[slot, h, me],
            device_id={"owners": w, "section": target}, device_id_type=MESH).start()

    def done(sem):
        pltpu.make_async_copy(bytes_of, bytes_of, sem).wait()

    def done_piece(sem):
        pltpu.make_async_copy(via.at[0], via.at[0], sem).wait()

    @pl.when(sec == 0)
    def _():
        for w in near:
            for h in range(span):
                send_a(x, 0, h, w, 0, s_in)
        for h in range(span):
            pltpu.make_async_copy(x.at[base + h], in_a.at[0, h, me], r_a.at[0, h, me]).start()

    @pl.when(sec != 0)
    def _():
        for d in range(n - 1, -1, -1):
            for h in range(span):
                send_a(x, sec + 1, h, lax.rem(me + d, n), 0, s_in)

    def weight_copy(src, dst, k):
        return pltpu.make_async_remote_copy(
            src_ref=src, dst_ref=dst,
            send_sem=s_w.at[k], recv_sem=r_w.at[k],
            device_id={"rep": 1 - rep}, device_id_type=MESH)

    weight_copy(w1, far1, 0).start()
    weight_copy(w2, far2, 1).start()

    def arrange(raw, til, links, begin, spans):
        radix = spans * blocks

        def one(b, carry):
            i = b + begin
            taken = [links[i, k] for k in range(radix)]
            for p in range(radix):
                slot = jnp.int32(0)
                for k in range(1, radix):
                    slot = jnp.where(taken[k] == p, k, slot)
                til[pl.ds(pl.multiple_of(i * tile, tile), tile), p * tile:(p + 1) * tile] = raw[b, slot].T
            return carry

        lax.fori_loop(0, half, one, 0)

    def bias_columns(b, col):
        for i in range(blocks):
            row = b[0:1, i * tile:(i + 1) * tile]
            col[i * tile:(i + 1) * tile, :] = jnp.broadcast_to(row, (rows, tile)).T

    for copy in local[2:]:
        copy.wait()
    bias_columns(b1, col1)
    bias_columns(b2, col2)
    local[0].wait()
    arrange(raw1, til1, l1, rep * half, span)
    weight_copy(w1, far1, 0).wait_recv()
    arrange(far1, til1, l1, (1 - rep) * half, span)

    def slab(ref, w):
        return ref[pl.ds(pl.multiple_of(w * piece, piece), piece), :]

    def product(til, v, col, w):
        part = jnp.dot(slab(til, w), v, preferred_element_type=jnp.float32)
        return jnp.clip(part + slab(col, w), 0.0, CEILING).astype(jnp.bfloat16)

    def far(d):
        low, high = me, n - 1 - me
        short = jnp.minimum(low, high)
        k = n - 1 - d
        both = (k + 1) // 2
        away = jnp.where(k <= 2 * short, both, k - short)
        up = jnp.where(k <= 2 * short, (k % 2) == 0, high > low)
        return jnp.where(up, me + away, me - away)

    def slot_of(m):
        return jnp.where(sec == 0, 0, 1) if m == 0 else m + 1

    def forward(m, h, u, j):
        slot = slot_of(m)
        return pltpu.make_async_remote_copy(
            src_ref=in_a.at[slot, h, u], dst_ref=in_a.at[slot, h, u],
            send_sem=s_f.at[m, h, u, j - 1], recv_sem=r_a.at[slot, h, u],
            device_id={"owners": mate(j)}, device_id_type=MESH)

    def relayed(m, k, act):
        if m == last:
            if m == 0 and k > 0:
                pl.when(sec == 0)(act)
        elif m == 0 and k > 0:
            act()
        else:
            pl.when(sec > 0)(act)

    def forwards(m, act):
        for k in range(classes):
            def go():
                for h in range(span):
                    for j in range(1, span):
                        act(forward(m, h, fellow(k), j))
            relayed(m, k, go)

    def first_layer(m):
        slot = slot_of(m)
        def pull(u, passing):
            for h in range(span):
                done(r_a.at[slot, h, u])
                if passing:
                    for j in range(1, span):
                        forward(m, h, u, j).start()

        @pl.when(sec == 0)
        def _():
            for k in range(classes):
                pull(fellow(k), m == 0 and k > 0)

        @pl.when(sec > 0)
        def _():
            edge = jnp.logical_or(me == 0, me == n - 1)
            if m == 0:
                @pl.when(jnp.logical_and(sec == 1, edge))
                def _():
                    pass_on(True)
            for k in range(classes):
                if m == 0 and k == classes - 1:
                    @pl.when(jnp.logical_and(sec == 1, jnp.logical_not(edge)))
                    def _():
                        pass_on(True)
                pull(fellow(jnp.where(edge, k, classes - 1 - k)), m < last)

        for j in range(1, span):
            for k in range(classes):
                for h in range(span):
                    done(r_a.at[slot, h, lax.rem(mate(j) + span * k, n)])
        v = in_a[slot].reshape(span * width, rows)
        for d in range(n):
            w = far(d)
            mid[m, w] = product(til1, v, col1, w)
            if d < n - 1:
                def straight():
                    pltpu.make_async_remote_copy(
                        src_ref=mid.at[m, w], dst_ref=in_b.at[m, me],
                        send_sem=s_b.at[m, d + 1], recv_sem=r_b.at[m, me],
                        device_id={"owners": w}, device_id_type=MESH).start()

                def detour():
                    pltpu.make_async_remote_copy(
                        src_ref=mid.at[m, w], dst_ref=via.at[w],
                        send_sem=s_b.at[m, d + 1], recv_sem=r_v.at[w],
                        device_id={"section": 1}, device_id_type=MESH).start()

                if m == 1:
                    pl.when(sec == 0)(detour)
                    pl.when(sec > 0)(straight)
                else:
                    straight()
            else:
                in_b[m, me] = mid[m, me]

    def home(m, first):
        part = pl.ds(first, span)
        return pltpu.make_async_remote_copy(
            src_ref=res.at[m, part], dst_ref=o.at[part], send_sem=s_o.at[m, first // span], recv_sem=r_o.at[first // span],
            device_id={"section": m}, device_id_type=MESH)

    def second_layer(m):
        for d in range(1, n):
            done(r_b.at[m, lax.rem(me + d, n)])
        v = in_b[m].reshape(width, rows)
        for d in range(n - span, -1, -span):
            w = lax.rem(me + d, n)
            first = w - lax.rem(w, span)
            for h in range(span):
                value = product(til2, v, col2, first + h)
                res[m, first + h] = value
                if m == last:
                    @pl.when(sec == last)
                    def _():
                        o[first + h] = value

            if last > 0:
                @pl.when(sec < last)
                def _():
                    for j in range(span if m == last else 1):
                        for h in range(span):
                            send_a(res.at[m], m + 1, h, first + lax.rem(w - first + j, span), sec + 1, s_a.at[m])

            if m < last:
                @pl.when(sec == last)
                def _():
                    home(m, first).start()

    def arrange_second():
        local[1].wait()
        arrange(raw2, til2, l2, rep * half, 1)
        weight_copy(w2, far2, 1).wait_recv()
        arrange(far2, til2, l2, (1 - rep) * half, 1)

    def onward(w):
        return pltpu.make_async_remote_copy(
            src_ref=via.at[w], dst_ref=in_b.at[1, me], send_sem=s_v.at[w], recv_sem=r_b.at[1, me],
            device_id={"owners": w, "section": 0}, device_id_type=MESH)

    @pl.when(sec > 0)
    def _():
        arrange_second()

    def apart(w):
        return jnp.logical_or(w < base, w >= base + span)

    def pass_on(near_ones):
        for d in range(n - 1):
            w = far(d)

            @pl.when(jnp.logical_xor(apart(w), near_ones))
            def _():
                done_piece(r_v.at[w])
                onward(w).start()

    if last > 0:
        @pl.when(sec == 1)
        def _():
            pass_on(False)

    first_layer(0)

    if last > 0:
        @pl.when(sec == 0)
        def _():
            pl.semaphore_wait(ready, classes)

    for m in range(sections):
        if m < last:
            @pl.when(sec == 0)
            def _():
                first_layer(m + 1)
        if m == 0:
            @pl.when(sec == 0)
            def _():
                arrange_second()
        second_layer(m)
        if m < last:
            @pl.when(sec > 0)
            def _():
                first_layer(m + 1)

    def sent(ref, sem):
        pltpu.make_async_copy(ref, ref, sem).wait()

    @pl.when(sec == 0)
    def _():
        for w in near:
            for h in range(span):
                done(s_in.at[h, w])

    @pl.when(sec != 0)
    def _():
        for w in range(n):
            for h in range(span):
                done(s_in.at[h, w])
    for m in range(sections):
        forwards(m, lambda copy: copy.wait_send())
        for d in range(1, n):
            sent(mid.at[m, 0], s_b.at[m, d])
    weight_copy(w1, far1, 0).wait_send()
    weight_copy(w2, far2, 1).wait_send()
    if last > 0:
        @pl.when(sec == 1)
        def _():
            for d in range(n - 1):
                onward(far(d)).wait_send()

        @pl.when(sec < last)
        def _():
            for m in range(sections):
                for d in range(0, n, 1 if m == last else span):
                    for h in range(span):
                        done(s_a.at[m, h, lax.rem(me + d, n)])
            for k in range(classes):
                sent(o.at[pl.ds(0, span)], r_o.at[k])

        @pl.when(sec == last)
        def _():
            for m in range(last):
                for k in range(classes):
                    home(m, k * span).wait_send()


def body(inputs, weight_first, weight_second, bias_first, bias_second, links_first, links_second):
    n = lax.axis_size("owners")
    sections = lax.axis_size("section")
    width, rows = inputs.shape[1:]
    half, deep, tile = weight_first.shape[1:]
    radix_a = links_first.shape[2]
    radix_b = links_second.shape[2]
    blocks = width // tile
    span = radix_a // blocks
    piece = width // n
    dims = (n, sections, span, tile)
    bf = jnp.bfloat16
    anyspace = pl.BlockSpec(memory_space=pltpu.HBM)
    vmem = pl.BlockSpec(memory_space=pltpu.VMEM)
    dma = pltpu.SemaphoreType.DMA
    out = pl.pallas_call(
        functools.partial(relay, dims),
        name="relay",
        out_shape=pltpu.VMEM((n, piece, rows), bf),
        in_specs=[anyspace] * 7,
        out_specs=vmem,
        scratch_shapes=[
            pltpu.VMEM(bias_first.shape, jnp.float32),
            pltpu.VMEM(bias_second.shape, jnp.float32),
            pltpu.SMEM(links_first.shape[1:], jnp.int32),
            pltpu.SMEM(links_second.shape[1:], jnp.int32),
            pltpu.VMEM((half, radix_a, tile, tile), bf),
            pltpu.VMEM((half, radix_a, tile, tile), bf),
            pltpu.VMEM((half, radix_b, tile, tile), bf),
            pltpu.VMEM((half, radix_b, tile, tile), bf),
            pltpu.VMEM((width, radix_a * tile), bf),
            pltpu.VMEM((width, radix_b * tile), bf),
            pltpu.VMEM((width, rows), jnp.float32),
            pltpu.VMEM((width, rows), jnp.float32),
            pltpu.VMEM((sections + 1, span, n, piece, rows), bf),
            pltpu.VMEM((sections, n, piece, rows), bf),
            pltpu.VMEM((sections, n, piece, rows), bf),
            pltpu.VMEM((sections, n, piece, rows), bf),
            pltpu.VMEM((n, piece, rows), bf),
            dma((2,)), dma((2,)), dma((6,)),
            dma((span, n)), dma((sections, span, n)), dma((sections + 1, span, n)),
            dma((sections, span, n, max(span - 1, 1))),
            dma((sections, n)), dma((sections, n)),
            dma((sections, n // span)), dma((n // span,)), dma((n,)), dma((n,)), pltpu.SemaphoreType.REGULAR,
        ],
        compiler_params=pltpu.CompilerParams(
            collective_id=0, has_side_effects=True, vmem_limit_bytes=63 * 2 ** 20 + 2 ** 19),
    )(
        inputs.reshape(n, piece, rows),
        weight_first.reshape(half, radix_a, tile, tile),
        weight_second.reshape(half, radix_b, tile, tile),
        bias_first, bias_second, links_first[0], links_second[0],
    )
    return out.reshape(1, width, rows)


def solution(mesh):
    placed = (
        P("section", "owners", ("groups", "rep")),
        P("section", ("owners", "rep"), None, None),
        P("section", ("owners", "rep"), None, None),
        P("section", "owners"),
        P("section", "owners"),
        P("section", "owners", None),
        P("section", "owners", None),
    )
    return jax.shard_map(
        body,
        mesh=mesh,
        in_specs=placed,
        out_specs=P("section", "owners", ("groups", "rep")),
        check_vma=False,
    )
```

```python
import functools

import jax
import jax.numpy as jnp
from jax import lax
from jax.experimental import pallas as pl
from jax.experimental.pallas import tpu as pltpu
from jax.sharding import PartitionSpec as P

CEILING = 4.0
MESH = pl.DeviceIdType.MESH


def relay(dims, x, w1, w2, b1_in, b2_in, l1_in, l2_in, o, b1, b2, l1, l2, raw1, far1, raw2, far2, til1, til2, col1, col2,
          in_a, in_b, mid, res, via, acc, s_w, r_w, l_w, s_in, s_a, r_a, s_f, s_b, r_b, s_o, r_o, s_v, r_v, ready):
    n, sections, span, tile = dims
    me = lax.axis_index("owners")
    sec = lax.axis_index("section")
    rep = lax.axis_index("rep")
    piece = x.shape[1]
    width = n * piece
    rows = x.shape[2]
    blocks = width // tile
    half = w1.shape[0]
    last = sections - 1

    barrier = pltpu.get_barrier_semaphore()
    par = lax.rem(me, span)
    base = me - par
    classes = n // span

    def fellow(k):
        return lax.rem(me + span * k, n)

    def mate(j):
        return base + lax.rem(par + j, span)

    def greet(sem, w, t):
        pl.semaphore_signal(sem, inc=1, device_id={"owners": w, "section": t}, device_id_type=MESH)

    near = [fellow(k) for k in range(1, classes)] + [mate(j) for j in range(1, span)]

    @pl.when(sec == 0)
    def _():
        for w in near:
            greet(barrier, w, 0)
    for t in range(1, sections):
        for w in range(n):
            @pl.when(jnp.logical_or(me != w, sec != t))
            def _():
                greet(barrier, w, t)
    pl.semaphore_signal(barrier, inc=1, device_id={"rep": 1 - rep}, device_id_type=MESH)

    local = [
        pltpu.make_async_copy(w1, raw1, l_w.at[0]),
        pltpu.make_async_copy(w2, raw2, l_w.at[1]),
        pltpu.make_async_copy(l1_in, l1, l_w.at[2]),
        pltpu.make_async_copy(l2_in, l2, l_w.at[3]),
        pltpu.make_async_copy(b1_in, b1, l_w.at[4]),
        pltpu.make_async_copy(b2_in, b2, l_w.at[5]),
    ]
    for copy in local:
        copy.start()
    @pl.when(sec == 0)
    def _():
        pl.semaphore_wait(barrier, len(near) + 1)

    @pl.when(sec != 0)
    def _():
        pl.semaphore_wait(barrier, n * sections)

    @pl.when(sec == 1)
    def _():
        for k in range(classes):
            greet(ready, fellow(k), 0)

    bytes_of = in_a.at[0, 0, 0]

    def send_a(src, slot, h, w, target, sem):
        pltpu.make_async_remote_copy(
            src_ref=src.at[(w // span) * span + h], dst_ref=in_a.at[slot, h, me],
            send_sem=sem.at[h, w], recv_sem=r_a.at[slot, h, me],
            device_id={"owners": w, "section": target}, device_id_type=MESH).start()

    def done(sem):
        pltpu.make_async_copy(bytes_of, bytes_of, sem).wait()

    def done_piece(sem):
        pltpu.make_async_copy(via.at[0], via.at[0], sem).wait()

    @pl.when(sec == 0)
    def _():
        for w in near:
            for h in range(span):
                send_a(x, 0, h, w, 0, s_in)
        for h in range(span):
            pltpu.make_async_copy(x.at[base + h], in_a.at[0, h, me], r_a.at[0, h, me]).start()

    @pl.when(sec != 0)
    def _():
        for d in range(n - 1, -1, -1):
            for h in range(span):
                send_a(x, sec + 1, h, lax.rem(me + d, n), 0, s_in)

    def weight_copy(src, dst, k):
        return pltpu.make_async_remote_copy(
            src_ref=src, dst_ref=dst,
            send_sem=s_w.at[k], recv_sem=r_w.at[k],
            device_id={"rep": 1 - rep}, device_id_type=MESH)

    weight_copy(w1, far1, 0).start()
    weight_copy(w2, far2, 1).start()

    def arrange(raw, til, links, begin, spans):
        radix = spans * blocks

        def one(b, carry):
            i = b + begin
            taken = [links[i, k] for k in range(radix)]
            for p in range(radix):
                slot = jnp.int32(0)
                for k in range(1, radix):
                    slot = jnp.where(taken[k] == p, k, slot)
                til[pl.ds(pl.multiple_of(i * tile, tile), tile), p * tile:(p + 1) * tile] = raw[b, slot].T
            return carry

        lax.fori_loop(0, half, one, 0)

    def bias_columns(b, col):
        for i in range(blocks):
            row = b[0:1, i * tile:(i + 1) * tile]
            col[i * tile:(i + 1) * tile, :] = jnp.broadcast_to(row, (rows, tile)).T

    for copy in local[2:]:
        copy.wait()
    bias_columns(b1, col1)
    bias_columns(b2, col2)
    local[0].wait()
    arrange(raw1, til1, l1, rep * half, span)
    weight_copy(w1, far1, 0).wait_recv()
    arrange(far1, til1, l1, (1 - rep) * half, span)

    def slab(ref, w):
        return ref[pl.ds(pl.multiple_of(w * piece, piece), piece), :]

    def bounds(part, col, w):
        return jnp.clip(part + slab(col, w), 0.0, CEILING).astype(jnp.bfloat16)

    def columns(til, height, u, spans):
        return jnp.concatenate(
            [til[height, pl.ds(pl.multiple_of(h * width + u * piece, tile), piece)] for h in range(spans)], axis=1)

    def gather_up(til, u, v, spans, fresh):
        part = jnp.dot(columns(til, slice(None), u, spans), v, preferred_element_type=jnp.float32)
        acc[...] = part if fresh else acc[...] + part

    def product(til, v, col, w, u, spans):
        if u is None:
            return bounds(jnp.dot(slab(til, w), v, preferred_element_type=jnp.float32), col, w)
        height = pl.ds(pl.multiple_of(w * piece, piece), piece)
        part = jnp.dot(columns(til, height, u, spans), v, preferred_element_type=jnp.float32)
        return bounds(slab(acc, w) + part, col, w)

    def far(d):
        low, high = me, n - 1 - me
        short = jnp.minimum(low, high)
        k = n - 1 - d
        both = (k + 1) // 2
        away = jnp.where(k <= 2 * short, both, k - short)
        up = jnp.where(k <= 2 * short, (k % 2) == 0, high > low)
        return jnp.where(up, me + away, me - away)

    def detour_order(d):
        other = mate(1) if span > 1 else far(0)
        at = sum(jnp.where(far(i) == other, i, 0) for i in range(n))
        w = other if d == 0 else jnp.where(d - 1 < at, far(d - 1), far(d))
        return jnp.where(sec == 0, w, far(d))

    def slot_of(m):
        return jnp.where(sec == 0, 0, 1) if m == 0 else m + 1

    def forward(m, h, u, j):
        slot = slot_of(m)
        return pltpu.make_async_remote_copy(
            src_ref=in_a.at[slot, h, u], dst_ref=in_a.at[slot, h, u],
            send_sem=s_f.at[m, h, u, j - 1], recv_sem=r_a.at[slot, h, u],
            device_id={"owners": mate(j)}, device_id_type=MESH)

    def relayed(m, k, act):
        if m == last:
            if m == 0 and k > 0:
                pl.when(sec == 0)(act)
        elif m == 0 and k > 0:
            act()
        else:
            pl.when(sec > 0)(act)

    def forwards(m, act):
        for k in range(classes):
            def go():
                for h in range(span):
                    for j in range(1, span):
                        act(forward(m, h, fellow(k), j))
            relayed(m, k, go)

    def first_layer(m):
        slot = slot_of(m)
        def pull(u, passing):
            for h in range(span):
                done(r_a.at[slot, h, u])
                if passing:
                    for j in range(1, span):
                        forward(m, h, u, j).start()

        @pl.when(sec == 0)
        def _():
            for k in range(classes):
                pull(fellow(k), m == 0 and k > 0)

        @pl.when(sec > 0)
        def _():
            edge = jnp.logical_or(me == 0, me == n - 1)
            for k in range(classes):
                pull(fellow(jnp.where(edge, k, classes - 1 - k)), m < last)

        turned = jnp.logical_and(sec > 0, jnp.logical_or(me == 0, me == n - 1))
        others = [
            lax.rem(mate(j) + span * (jnp.where(turned, classes - 1 - k, k) if m == 0 else k), n)
            for j in range(1, span) for k in range(classes)]
        sources = [fellow(k) for k in range(classes)] + others

        def landed(u):
            for h in range(span):
                done(r_a.at[slot, h, u])

        if piece % tile == 0 and n > 1 and m == 0:
            for i, u in enumerate(sources):
                if i >= classes:
                    landed(u)
                v = jnp.concatenate([in_a[slot, h, u] for h in range(span)], axis=0)
                if i < n - 1:
                    gather_up(til1, u, v, span, i == 0)
        else:
            for u in others:
                landed(u)
            u, v = None, in_a[slot].reshape(span * width, rows)
        for d in range(n):
            w = detour_order(d) if m == 1 else far(d)
            mid[m, w] = product(til1, v, col1, w, u, span)
            if d < n - 1:
                def straight():
                    pltpu.make_async_remote_copy(
                        src_ref=mid.at[m, w], dst_ref=in_b.at[m, me],
                        send_sem=s_b.at[m, d + 1], recv_sem=r_b.at[m, me],
                        device_id={"owners": w}, device_id_type=MESH).start()

                def detour():
                    pltpu.make_async_remote_copy(
                        src_ref=mid.at[m, w], dst_ref=via.at[w],
                        send_sem=s_b.at[m, d + 1], recv_sem=r_v.at[w],
                        device_id={"section": 1}, device_id_type=MESH).start()

                if m == 1:
                    pl.when(sec == 0)(detour)
                    pl.when(sec > 0)(straight)
                else:
                    straight()
            else:
                in_b[m, me] = mid[m, me]

    def home(m, first):
        part = pl.ds(first, span)
        return pltpu.make_async_remote_copy(
            src_ref=res.at[m, part], dst_ref=o.at[part], send_sem=s_o.at[m, first // span], recv_sem=r_o.at[first // span],
            device_id={"section": m}, device_id_type=MESH)

    def second_layer(m):
        if piece % tile == 0 and n > 1 and False:
            for i in range(n):
                u = far(n - 1 - i)
                if i > 0:
                    done(r_b.at[m, u])
                v = in_b[m, u]
                if i < n - 1:
                    gather_up(til2, u, v, 1, i == 0)
        else:
            for d in range(1, n):
                done(r_b.at[m, lax.rem(me + d, n)])
            u, v = None, in_b[m].reshape(width, rows)
        for d in range(n - span, -1, -span):
            w = lax.rem(me + d, n)
            first = w - lax.rem(w, span)
            for h in range(span):
                value = product(til2, v, col2, first + h, u, 1)
                res[m, first + h] = value
                if m == last:
                    @pl.when(sec == last)
                    def _():
                        o[first + h] = value

            if last > 0:
                @pl.when(sec < last)
                def _():
                    for j in range(span if m == last else 1):
                        for h in range(span):
                            send_a(res.at[m], m + 1, h, first + lax.rem(w - first + j, span), sec + 1, s_a.at[m])

            if m < last:
                @pl.when(sec == last)
                def _():
                    home(m, first).start()

    def arrange_second():
        local[1].wait()
        arrange(raw2, til2, l2, rep * half, 1)
        weight_copy(w2, far2, 1).wait_recv()
        arrange(far2, til2, l2, (1 - rep) * half, 1)

    def onward(w):
        return pltpu.make_async_remote_copy(
            src_ref=via.at[w], dst_ref=in_b.at[1, me], send_sem=s_v.at[w], recv_sem=r_b.at[1, me],
            device_id={"owners": w, "section": 0}, device_id_type=MESH)

    @pl.when(sec > 0)
    def _():
        arrange_second()

    def apart(w):
        return jnp.logical_or(w < base, w >= base + span)

    def pass_on(near_ones):
        for d in range(n - 1):
            w = far(d)

            @pl.when(jnp.logical_xor(apart(w), near_ones))
            def _():
                done_piece(r_v.at[w])
                onward(w).start()

    if last > 0:
        @pl.when(sec == 1)
        def _():
            pass_on(True)
            pass_on(False)

    first_layer(0)

    if last > 0:
        @pl.when(sec == 0)
        def _():
            pl.semaphore_wait(ready, classes)

    for m in range(sections):
        if m < last:
            @pl.when(sec == 0)
            def _():
                first_layer(m + 1)
        if m == 0:
            @pl.when(sec == 0)
            def _():
                arrange_second()
        second_layer(m)
        if m < last:
            @pl.when(sec > 0)
            def _():
                first_layer(m + 1)

    def sent(ref, sem):
        pltpu.make_async_copy(ref, ref, sem).wait()

    @pl.when(sec == 0)
    def _():
        for w in near:
            for h in range(span):
                done(s_in.at[h, w])

    @pl.when(sec != 0)
    def _():
        for w in range(n):
            for h in range(span):
                done(s_in.at[h, w])
    for m in range(sections):
        forwards(m, lambda copy: copy.wait_send())
        for d in range(1, n):
            sent(mid.at[m, 0], s_b.at[m, d])
    weight_copy(w1, far1, 0).wait_send()
    weight_copy(w2, far2, 1).wait_send()
    if last > 0:
        @pl.when(sec == 1)
        def _():
            for d in range(n - 1):
                onward(far(d)).wait_send()

        @pl.when(sec < last)
        def _():
            for m in range(sections):
                for d in range(0, n, 1 if m == last else span):
                    for h in range(span):
                        done(s_a.at[m, h, lax.rem(me + d, n)])
            for k in range(classes):
                sent(o.at[pl.ds(0, span)], r_o.at[k])

        @pl.when(sec == last)
        def _():
            for m in range(last):
                for k in range(classes):
                    home(m, k * span).wait_send()


def body(inputs, weight_first, weight_second, bias_first, bias_second, links_first, links_second):
    n = lax.axis_size("owners")
    sections = lax.axis_size("section")
    width, rows = inputs.shape[1:]
    half, deep, tile = weight_first.shape[1:]
    radix_a = links_first.shape[2]
    radix_b = links_second.shape[2]
    blocks = width // tile
    span = radix_a // blocks
    piece = width // n
    dims = (n, sections, span, tile)
    bf = jnp.bfloat16
    anyspace = pl.BlockSpec(memory_space=pltpu.HBM)
    vmem = pl.BlockSpec(memory_space=pltpu.VMEM)
    dma = pltpu.SemaphoreType.DMA
    out = pl.pallas_call(
        functools.partial(relay, dims),
        name="relay",
        out_shape=pltpu.VMEM((n, piece, rows), bf),
        in_specs=[anyspace] * 7,
        out_specs=vmem,
        scratch_shapes=[
            pltpu.VMEM(bias_first.shape, jnp.float32),
            pltpu.VMEM(bias_second.shape, jnp.float32),
            pltpu.SMEM(links_first.shape[1:], jnp.int32),
            pltpu.SMEM(links_second.shape[1:], jnp.int32),
            pltpu.VMEM((half, radix_a, tile, tile), bf),
            pltpu.VMEM((half, radix_a, tile, tile), bf),
            pltpu.VMEM((half, radix_b, tile, tile), bf),
            pltpu.VMEM((half, radix_b, tile, tile), bf),
            pltpu.VMEM((width, radix_a * tile), bf),
            pltpu.VMEM((width, radix_b * tile), bf),
            pltpu.VMEM((width, rows), jnp.float32),
            pltpu.VMEM((width, rows), jnp.float32),
            pltpu.VMEM((sections + 1, span, n, piece, rows), bf),
            pltpu.VMEM((sections, n, piece, rows), bf),
            pltpu.VMEM((sections, n, piece, rows), bf),
            pltpu.VMEM((sections, n, piece, rows), bf),
            pltpu.VMEM((n, piece, rows), bf),
            pltpu.VMEM((width, rows), jnp.float32),
            dma((2,)), dma((2,)), dma((6,)),
            dma((span, n)), dma((sections, span, n)), dma((sections + 1, span, n)),
            dma((sections, span, n, max(span - 1, 1))),
            dma((sections, n)), dma((sections, n)),
            dma((sections, n // span)), dma((n // span,)), dma((n,)), dma((n,)), pltpu.SemaphoreType.REGULAR,
        ],
        compiler_params=pltpu.CompilerParams(
            collective_id=0, has_side_effects=True, vmem_limit_bytes=63 * 2 ** 20 + 2 ** 19),
    )(
        inputs.reshape(n, piece, rows),
        weight_first.reshape(half, radix_a, tile, tile),
        weight_second.reshape(half, radix_b, tile, tile),
        bias_first, bias_second, links_first[0], links_second[0],
    )
    return out.reshape(1, width, rows)


def solution(mesh):
    placed = (
        P("section", "owners", ("groups", "rep")),
        P("section", ("owners", "rep"), None, None),
        P("section", ("owners", "rep"), None, None),
        P("section", "owners"),
        P("section", "owners"),
        P("section", "owners", None),
        P("section", "owners", None),
    )
    return jax.shard_map(
        body,
        mesh=mesh,
        in_specs=placed,
        out_specs=P("section", "owners", ("groups", "rep")),
        check_vma=False,
    )
```

```python
import functools

import jax
import jax.numpy as jnp
from jax import lax
from jax.experimental import pallas as pl
from jax.experimental.pallas import tpu as pltpu
from jax.sharding import PartitionSpec as P

CEILING = 4.0
MESH = pl.DeviceIdType.MESH


def relay(dims, x, w1, w2, b1_in, b2_in, l1_in, l2_in, o, b1, b2, l1, l2, raw1, far1, raw2, far2, til1, til2, col1, col2,
          in_a, in_b, mid, res, via, acc, s_w, r_w, l_w, s_in, s_a, r_a, s_f, s_b, r_b, s_o, r_o, s_v, r_v, ready):
    n, sections, span, tile = dims
    me = lax.axis_index("owners")
    sec = lax.axis_index("section")
    rep = lax.axis_index("rep")
    piece = x.shape[1]
    width = n * piece
    rows = x.shape[2]
    blocks = width // tile
    half = w1.shape[0]
    last = sections - 1

    barrier = pltpu.get_barrier_semaphore()
    par = lax.rem(me, span)
    base = me - par
    classes = n // span

    def fellow(k):
        return lax.rem(me + span * k, n)

    def mate(j):
        return base + lax.rem(par + j, span)

    def greet(sem, w, t):
        pl.semaphore_signal(sem, inc=1, device_id={"owners": w, "section": t}, device_id_type=MESH)

    near = [fellow(k) for k in range(1, classes)] + [mate(j) for j in range(1, span)]

    @pl.when(sec == 0)
    def _():
        for w in near:
            greet(barrier, w, 0)
    for t in range(1, sections):
        for w in range(n):
            @pl.when(jnp.logical_or(me != w, sec != t))
            def _():
                greet(barrier, w, t)
    pl.semaphore_signal(barrier, inc=1, device_id={"rep": 1 - rep}, device_id_type=MESH)

    local = [
        pltpu.make_async_copy(w1, raw1, l_w.at[0]),
        pltpu.make_async_copy(w2, raw2, l_w.at[1]),
        pltpu.make_async_copy(l1_in, l1, l_w.at[2]),
        pltpu.make_async_copy(l2_in, l2, l_w.at[3]),
        pltpu.make_async_copy(b1_in, b1, l_w.at[4]),
        pltpu.make_async_copy(b2_in, b2, l_w.at[5]),
    ]
    for copy in local:
        copy.start()
    @pl.when(sec == 0)
    def _():
        pl.semaphore_wait(barrier, len(near) + 1)

    @pl.when(sec != 0)
    def _():
        pl.semaphore_wait(barrier, n * sections)

    @pl.when(sec == 1)
    def _():
        for k in range(classes):
            greet(ready, fellow(k), 0)

    bytes_of = in_a.at[0, 0, 0]

    def send_a(src, slot, h, w, target, sem):
        pltpu.make_async_remote_copy(
            src_ref=src.at[(w // span) * span + h], dst_ref=in_a.at[slot, h, me],
            send_sem=sem.at[h, w], recv_sem=r_a.at[slot, h, me],
            device_id={"owners": w, "section": target}, device_id_type=MESH).start()

    def done(sem):
        pltpu.make_async_copy(bytes_of, bytes_of, sem).wait()

    def done_piece(sem):
        pltpu.make_async_copy(via.at[0], via.at[0], sem).wait()

    @pl.when(sec == 0)
    def _():
        for w in near:
            for h in range(span):
                send_a(x, 0, h, w, 0, s_in)
        for h in range(span):
            pltpu.make_async_copy(x.at[base + h], in_a.at[0, h, me], r_a.at[0, h, me]).start()

    @pl.when(sec != 0)
    def _():
        for d in range(n - 1, -1, -1):
            for h in range(span):
                send_a(x, sec + 1, h, lax.rem(me + d, n), 0, s_in)

    def weight_copy(src, dst, k):
        return pltpu.make_async_remote_copy(
            src_ref=src, dst_ref=dst,
            send_sem=s_w.at[k], recv_sem=r_w.at[k],
            device_id={"rep": 1 - rep}, device_id_type=MESH)

    weight_copy(w1, far1, 0).start()
    weight_copy(w2, far2, 1).start()

    def arrange(raw, til, links, begin, spans):
        radix = spans * blocks

        def one(b, carry):
            i = b + begin
            taken = [links[i, k] for k in range(radix)]
            for p in range(radix):
                slot = jnp.int32(0)
                for k in range(1, radix):
                    slot = jnp.where(taken[k] == p, k, slot)
                til[pl.ds(pl.multiple_of(i * tile, tile), tile), p * tile:(p + 1) * tile] = raw[b, slot].T
            return carry

        lax.fori_loop(0, half, one, 0)

    def bias_columns(b, col):
        for i in range(blocks):
            row = b[0:1, i * tile:(i + 1) * tile]
            col[i * tile:(i + 1) * tile, :] = jnp.broadcast_to(row, (rows, tile)).T

    for copy in local[2:]:
        copy.wait()
    bias_columns(b1, col1)
    bias_columns(b2, col2)
    local[0].wait()
    arrange(raw1, til1, l1, rep * half, span)
    weight_copy(w1, far1, 0).wait_recv()
    arrange(far1, til1, l1, (1 - rep) * half, span)

    def slab(ref, w):
        return ref[pl.ds(pl.multiple_of(w * piece, piece), piece), :]

    def bounds(part, col, w):
        return jnp.clip(part + slab(col, w), 0.0, CEILING).astype(jnp.bfloat16)

    def columns(til, height, u, spans):
        return jnp.concatenate(
            [til[height, pl.ds(pl.multiple_of(h * width + u * piece, tile), piece)] for h in range(spans)], axis=1)

    def gather_up(til, u, v, spans, fresh):
        part = jnp.dot(columns(til, slice(None), u, spans), v, preferred_element_type=jnp.float32)
        acc[...] = part if fresh else acc[...] + part

    def product(til, v, col, w, u, spans):
        if u is None:
            return bounds(jnp.dot(slab(til, w), v, preferred_element_type=jnp.float32), col, w)
        height = pl.ds(pl.multiple_of(w * piece, piece), piece)
        part = jnp.dot(columns(til, height, u, spans), v, preferred_element_type=jnp.float32)
        return bounds(slab(acc, w) + part, col, w)

    def far(d):
        low, high = me, n - 1 - me
        short = jnp.minimum(low, high)
        k = n - 1 - d
        both = (k + 1) // 2
        away = jnp.where(k <= 2 * short, both, k - short)
        up = jnp.where(k <= 2 * short, (k % 2) == 0, high > low)
        return jnp.where(up, me + away, me - away)

    def detour_order(d):
        other = mate(1) if span > 1 else far(0)
        at = sum(jnp.where(far(i) == other, i, 0) for i in range(n))
        w = other if d == 0 else jnp.where(d - 1 < at, far(d - 1), far(d))
        return jnp.where(sec == 0, w, far(d))

    def slot_of(m):
        return jnp.where(sec == 0, 0, 1) if m == 0 else m + 1

    def forward(m, h, u, j):
        slot = slot_of(m)
        return pltpu.make_async_remote_copy(
            src_ref=in_a.at[slot, h, u], dst_ref=in_a.at[slot, h, u],
            send_sem=s_f.at[m, h, u, j - 1], recv_sem=r_a.at[slot, h, u],
            device_id={"owners": mate(j)}, device_id_type=MESH)

    def relayed(m, k, act):
        if m == last:
            if m == 0 and k > 0:
                pl.when(sec == 0)(act)
        elif m == 0 and k > 0:
            act()
        else:
            pl.when(sec > 0)(act)

    def forwards(m, act):
        for k in range(classes):
            def go():
                for h in range(span):
                    for j in range(1, span):
                        act(forward(m, h, fellow(k), j))
            relayed(m, k, go)

    def first_layer(m):
        slot = slot_of(m)
        def pull(u, passing):
            for h in range(span):
                done(r_a.at[slot, h, u])
                if passing:
                    for j in range(1, span):
                        forward(m, h, u, j).start()

        @pl.when(sec == 0)
        def _():
            for k in range(classes):
                pull(fellow(k), m == 0 and k > 0)

        @pl.when(sec > 0)
        def _():
            edge = jnp.logical_or(me == 0, me == n - 1)
            for k in range(classes):
                pull(fellow(jnp.where(edge, k, classes - 1 - k)), m < last)

        turned = jnp.logical_and(sec > 0, jnp.logical_or(me == 0, me == n - 1))
        others = [
            lax.rem(mate(j) + span * (jnp.where(turned, classes - 1 - k, k) if m == 0 else k), n)
            for j in range(1, span) for k in range(classes)]
        sources = [fellow(k) for k in range(classes)] + others

        def landed(u):
            for h in range(span):
                done(r_a.at[slot, h, u])

        if piece % tile == 0 and n > 1 and m == 0:
            for i, u in enumerate(sources):
                if i >= classes:
                    landed(u)
                v = jnp.concatenate([in_a[slot, h, u] for h in range(span)], axis=0)
                if i < n - 1:
                    gather_up(til1, u, v, span, i == 0)
        else:
            for u in others:
                landed(u)
            u, v = None, in_a[slot].reshape(span * width, rows)
        for d in range(n):
            w = detour_order(d) if m == 1 else far(d)
            mid[m, w] = product(til1, v, col1, w, u, span)
            if d < n - 1:
                def straight():
                    pltpu.make_async_remote_copy(
                        src_ref=mid.at[m, w], dst_ref=in_b.at[m, me],
                        send_sem=s_b.at[m, d + 1], recv_sem=r_b.at[m, me],
                        device_id={"owners": w}, device_id_type=MESH).start()

                def detour():
                    pltpu.make_async_remote_copy(
                        src_ref=mid.at[m, w], dst_ref=via.at[w],
                        send_sem=s_b.at[m, d + 1], recv_sem=r_v.at[w],
                        device_id={"section": 1}, device_id_type=MESH).start()

                if m == 1:
                    pl.when(sec == 0)(detour)
                    pl.when(sec > 0)(straight)
                else:
                    straight()
            else:
                in_b[m, me] = mid[m, me]

    def home(m, first):
        part = pl.ds(first, span)
        return pltpu.make_async_remote_copy(
            src_ref=res.at[m, part], dst_ref=o.at[part], send_sem=s_o.at[m, first // span], recv_sem=r_o.at[first // span],
            device_id={"section": m}, device_id_type=MESH)

    def second_layer(m):
        if piece % tile == 0 and n > 1 and m == last:
            for i in range(n):
                u = far(n - 1 - i)
                if i > 0:
                    done(r_b.at[m, u])
                v = in_b[m, u]
                if i < n - 1:
                    gather_up(til2, u, v, 1, i == 0)
        else:
            for d in range(1, n):
                done(r_b.at[m, lax.rem(me + d, n)])
            u, v = None, in_b[m].reshape(width, rows)
        for d in range(n - span, -1, -span):
            w = lax.rem(me + d, n)
            first = w - lax.rem(w, span)
            for h in range(span):
                value = product(til2, v, col2, first + h, u, 1)
                res[m, first + h] = value
                if m == last:
                    @pl.when(sec == last)
                    def _():
                        o[first + h] = value

            if last > 0:
                @pl.when(sec < last)
                def _():
                    for j in range(span if m == last else 1):
                        for h in range(span):
                            send_a(res.at[m], m + 1, h, first + lax.rem(w - first + j, span), sec + 1, s_a.at[m])

            if m < last:
                @pl.when(sec == last)
                def _():
                    home(m, first).start()

    def arrange_second():
        local[1].wait()
        arrange(raw2, til2, l2, rep * half, 1)
        weight_copy(w2, far2, 1).wait_recv()
        arrange(far2, til2, l2, (1 - rep) * half, 1)

    def onward(w):
        return pltpu.make_async_remote_copy(
            src_ref=via.at[w], dst_ref=in_b.at[1, me], send_sem=s_v.at[w], recv_sem=r_b.at[1, me],
            device_id={"owners": w, "section": 0}, device_id_type=MESH)

    @pl.when(sec > 0)
    def _():
        arrange_second()

    def apart(w):
        return jnp.logical_or(w < base, w >= base + span)

    def pass_on(near_ones):
        for d in range(n - 1):
            w = far(d)

            @pl.when(jnp.logical_xor(apart(w), near_ones))
            def _():
                done_piece(r_v.at[w])
                onward(w).start()

    if last > 0:
        @pl.when(sec == 1)
        def _():
            pass_on(True)
            pass_on(False)

    first_layer(0)

    if last > 0:
        @pl.when(sec == 0)
        def _():
            pl.semaphore_wait(ready, classes)

    def sent(ref, sem):
        pltpu.make_async_copy(ref, ref, sem).wait()

    def settle_sends():
        @pl.when(sec == 0)
        def _():
            for w in near:
                for h in range(span):
                    done(s_in.at[h, w])

        @pl.when(sec != 0)
        def _():
            for w in range(n):
                for h in range(span):
                    done(s_in.at[h, w])
        for m in range(sections):
            forwards(m, lambda copy: copy.wait_send())
            for d in range(1, n if m < last else 1):
                sent(mid.at[m, 0], s_b.at[m, d])
        weight_copy(w1, far1, 0).wait_send()
        weight_copy(w2, far2, 1).wait_send()
        if last > 0:
            @pl.when(sec == 1)
            def _():
                for d in range(n - 1):
                    onward(far(d)).wait_send()

    for m in range(sections):
        if m < last:
            @pl.when(sec == 0)
            def _():
                first_layer(m + 1)
        if m == 0:
            @pl.when(sec == 0)
            def _():
                arrange_second()
        if m == last:
            settle_sends()
        second_layer(m)
        if m < last:
            @pl.when(sec > 0)
            def _():
                first_layer(m + 1)

    for d in range(1, n):
        sent(mid.at[last, 0], s_b.at[last, d])
    if last > 0:
        @pl.when(sec < last)
        def _():
            for m in range(sections):
                for d in range(0, n, 1 if m == last else span):
                    for h in range(span):
                        done(s_a.at[m, h, lax.rem(me + d, n)])
            for k in range(classes):
                sent(o.at[pl.ds(0, span)], r_o.at[k])

        @pl.when(sec == last)
        def _():
            for m in range(last):
                for k in range(classes):
                    home(m, k * span).wait_send()


def body(inputs, weight_first, weight_second, bias_first, bias_second, links_first, links_second):
    n = lax.axis_size("owners")
    sections = lax.axis_size("section")
    width, rows = inputs.shape[1:]
    half, deep, tile = weight_first.shape[1:]
    radix_a = links_first.shape[2]
    radix_b = links_second.shape[2]
    blocks = width // tile
    span = radix_a // blocks
    piece = width // n
    dims = (n, sections, span, tile)
    bf = jnp.bfloat16
    anyspace = pl.BlockSpec(memory_space=pltpu.HBM)
    vmem = pl.BlockSpec(memory_space=pltpu.VMEM)
    dma = pltpu.SemaphoreType.DMA
    out = pl.pallas_call(
        functools.partial(relay, dims),
        name="relay",
        out_shape=pltpu.VMEM((n, piece, rows), bf),
        in_specs=[anyspace] * 7,
        out_specs=vmem,
        scratch_shapes=[
            pltpu.VMEM(bias_first.shape, jnp.float32),
            pltpu.VMEM(bias_second.shape, jnp.float32),
            pltpu.SMEM(links_first.shape[1:], jnp.int32),
            pltpu.SMEM(links_second.shape[1:], jnp.int32),
            pltpu.VMEM((half, radix_a, tile, tile), bf),
            pltpu.VMEM((half, radix_a, tile, tile), bf),
            pltpu.VMEM((half, radix_b, tile, tile), bf),
            pltpu.VMEM((half, radix_b, tile, tile), bf),
            pltpu.VMEM((width, radix_a * tile), bf),
            pltpu.VMEM((width, radix_b * tile), bf),
            pltpu.VMEM((width, rows), jnp.float32),
            pltpu.VMEM((width, rows), jnp.float32),
            pltpu.VMEM((sections + 1, span, n, piece, rows), bf),
            pltpu.VMEM((sections, n, piece, rows), bf),
            pltpu.VMEM((sections, n, piece, rows), bf),
            pltpu.VMEM((sections, n, piece, rows), bf),
            pltpu.VMEM((n, piece, rows), bf),
            pltpu.VMEM((width, rows), jnp.float32),
            dma((2,)), dma((2,)), dma((6,)),
            dma((span, n)), dma((sections, span, n)), dma((sections + 1, span, n)),
            dma((sections, span, n, max(span - 1, 1))),
            dma((sections, n)), dma((sections, n)),
            dma((sections, n // span)), dma((n // span,)), dma((n,)), dma((n,)), pltpu.SemaphoreType.REGULAR,
        ],
        compiler_params=pltpu.CompilerParams(
            collective_id=0, has_side_effects=True, vmem_limit_bytes=63 * 2 ** 20 + 2 ** 19),
    )(
        inputs.reshape(n, piece, rows),
        weight_first.reshape(half, radix_a, tile, tile),
        weight_second.reshape(half, radix_b, tile, tile),
        bias_first, bias_second, links_first[0], links_second[0],
    )
    return out.reshape(1, width, rows)


def solution(mesh):
    placed = (
        P("section", "owners", ("groups", "rep")),
        P("section", ("owners", "rep"), None, None),
        P("section", ("owners", "rep"), None, None),
        P("section", "owners"),
        P("section", "owners"),
        P("section", "owners", None),
        P("section", "owners", None),
    )
    return jax.shard_map(
        body,
        mesh=mesh,
        in_specs=placed,
        out_specs=P("section", "owners", ("groups", "rep")),
        check_vma=False,
    )
```
